256 devices in a mesh: chan: 32 (over z, x_hi, core), row: 4 (over y), col: 2 (over x_lo).
Axes of the slice: x: 4 (x_hi: 2, x_lo: 2; x = x_hi * 2 + x_lo), y: 4, z: 8, core: 2. Of those that a mesh axis runs over, the one named last changes fastest.
Arguments:
- voltages: bfloat16 [1024, 262144], P('chan', ('row', 'col')), may hold values from -6 to 6
Outputs:
- visibilities: float32 [256, 2, 1024, 1024], P('chan', None, 'row', 'col')
The draws below stay inside these ranges and needn't reach their ends.
All inputs are finite; a program needn't handle non-finite values.
Results may differ from the reference program's by a relative error of at most 0.0053.
Values may be sent and summed in bfloat16 or wider, within the bound.
No kernel may reach another device: no remote copies, remote signals or barrier semaphores. Data moves between devices by JAX's collectives and lax.ppermute only.
A program may use at most 128 MiB of HBM per device.

```python
import jax
import jax.numpy as jnp
from jax import lax

INPUTS = 1024
FFT_LEN = 512
TAPS = 8
CHANNELS = 256
SPECTRA = 512
N_CHAN = 32


def shard_levels(rng, dims, shards, low, largest):
    factor_of, own = 1.0, jax.random.fold_in(rng, 6)
    for dim, blocks in shards:
        heights = jnp.exp(jax.random.uniform(jax.random.fold_in(own, dim), (blocks,), jnp.float32, low / len(shards), largest / len(shards)))
        factor_of = factor_of * jnp.repeat(heights, dims[dim] // blocks).reshape([-1 if axis == dim else 1 for axis in range(len(dims))])
    return factor_of


def gaussian(own_key, shape, spread, bound, cuts=(), kind=jnp.bfloat16):
    level = shard_levels(own_key, shape, cuts, -0.22, 0.18) if cuts else 1.0
    drawn = jax.random.normal(own_key, shape, jnp.float32) * spread * level
    return jnp.minimum(jnp.maximum(drawn, -bound), bound).astype(kind)


def setup_inputs(seed: int = 0) -> dict:
    key_list = jax.random.split(jax.random.key(seed), 2)
    return {
        "voltages": gaussian(key_list[0], (INPUTS, SPECTRA * FFT_LEN), 1.0, 6.0, ((0, 32), (1, 8))),
    }


def window_table(taps, length):
    count = taps * length
    position = jnp.arange(count).astype(jnp.float32)
    offset = (position - count / 2 + 0.5) / length
    taper = 0.5 - 0.5 * jnp.cos(2.0 * jnp.pi * (position + 0.5) / count)
    values = jnp.sinc(offset) * taper
    values = values / jnp.sqrt(jnp.sum(values * values))
    return values.reshape(taps, length)

def fourier_table(channels, length):
    channel_index = jnp.arange(channels, dtype=jnp.int32)[:, None]
    sample_index = jnp.arange(length, dtype=jnp.int32)[None, :]
    phase = (channel_index * sample_index % length).astype(jnp.float32) * (2.0 * jnp.pi / length)
    return jnp.stack([jnp.cos(phase), -jnp.sin(phase)], axis=1).astype(jnp.bfloat16)

def reference(voltages):
    window = window_table(TAPS, FFT_LEN)
    table = fourier_table(CHANNELS, FFT_LEN).astype(jnp.float32)
    group = INPUTS // N_CHAN
    grouped = voltages.reshape(N_CHAN, group, SPECTRA * FFT_LEN)

    def analyse(block):
        zeros = jnp.zeros((group, (TAPS - 1) * FFT_LEN), jnp.bfloat16)
        padded = jnp.concatenate([zeros, block], axis=1).reshape(group, SPECTRA + TAPS - 1, FFT_LEN)
        total = jnp.zeros((group, SPECTRA, FFT_LEN), jnp.float32)
        for tap_index in range(TAPS):
            total = total + window[tap_index][None, None, :] * padded[:, tap_index:tap_index + SPECTRA, :].astype(jnp.float32)
        filtered = total.astype(jnp.bfloat16).astype(jnp.float32)
        spectra = jnp.einsum('kpn,isn->kpsi', table, filtered, precision=lax.Precision.HIGHEST)
        return spectra.astype(jnp.bfloat16)
    pieces = lax.map(analyse, grouped)
    spectra = jnp.transpose(pieces, (1, 2, 3, 0, 4)).reshape(CHANNELS, 2, SPECTRA, INPUTS)

    def correlate(single):
        values = single.astype(jnp.float32)
        stacked = values.reshape(2 * SPECTRA, INPUTS)
        flipped = jnp.concatenate([values[1], -values[0]], axis=0)
        real_part = jnp.dot(stacked.T, stacked, precision=lax.Precision.HIGHEST)
        imag_part = jnp.dot(flipped.T, stacked, precision=lax.Precision.HIGHEST)
        return jnp.stack([real_part, imag_part], axis=0) / SPECTRA
    return lax.map(correlate, spectra)
```

```python
import functools

import jax
import jax.numpy as jnp
import ml_dtypes
import numpy as np
from jax import lax
from jax.experimental import pallas as pl
from jax.experimental.pallas import tpu as pltpu
from jax.sharding import PartitionSpec as P

FFT_LEN = 512
TAPS = 8
CHANNELS = 256
LANES = 128


def window_table(taps, length):
    count = taps * length
    position = np.arange(count, dtype=np.float64)
    offset = (position - count / 2 + 0.5) / length
    taper = 0.5 - 0.5 * np.cos(2.0 * np.pi * (position + 0.5) / count)
    values = np.sinc(offset) * taper
    values = values / np.sqrt(np.sum(values * values))
    return values.reshape(taps, length).astype(np.float32)


def fourier_table(channels, length):
    channel_index = np.arange(channels)[:, None]
    sample_index = np.arange(length)[None, :]
    phase = (channel_index * sample_index % length) * (2.0 * np.pi / length)
    return np.stack([np.cos(phase), -np.sin(phase)]).astype(np.float32).astype(ml_dtypes.bfloat16)


def channelize_kernel(v_ref, h_ref, w_ref, tab_ref, o_ref, f_ref, t_ref):
    inputs = v_ref.shape[0]
    spectra = v_ref.shape[1] // FFT_LEN
    row_tile = 16
    n_chunks = FFT_LEN // LANES

    def fir(step, carry):
        first_row = pl.multiple_of((step // n_chunks) * row_tile, row_tile)
        chunk = step % n_chunks
        lane = pl.multiple_of(chunk * LANES, LANES)
        rows = pl.ds(first_row, row_tile)
        taps = [w_ref[t : t + 1, pl.ds(lane, LANES)] for t in range(TAPS)]
        taps = [jnp.broadcast_to(t, (row_tile, LANES)) for t in taps]
        sums = {}
        for block in range(spectra + TAPS - 1):
            if block < TAPS - 1:
                value = h_ref[rows, pl.ds(block * FFT_LEN + lane, LANES)]
            else:
                value = v_ref[rows, pl.ds((block - TAPS + 1) * FFT_LEN + lane, LANES)]
            value = value.astype(jnp.float32)
            for t in range(TAPS):
                s = block - t
                if 0 <= s < spectra:
                    term = taps[t] * value
                    sums[s] = term if t == 0 else sums[s] + term
            done = block - TAPS + 1
            if done >= 0:
                f_ref[chunk, pl.ds(first_row * spectra + done, row_tile, stride=spectra), :] = sums.pop(done)
        return carry

    lax.fori_loop(0, (inputs // row_tile) * n_chunks, fir, 0)

    group = 8
    low = lax.broadcasted_iota(jnp.int32, (CHANNELS, LANES), 1) < spectra

    def dft(step, carry):
        start = pl.multiple_of(step * group * spectra, group * spectra)
        rows = pl.ds(start, group * spectra)
        block = jnp.concatenate([f_ref[c, rows, :].astype(jnp.bfloat16) for c in range(n_chunks)], axis=1)
        dims = (((1,), (1,)), ((), ()))
        real = lax.dot_general(tab_ref[0], block, dims, preferred_element_type=jnp.float32)
        imag = lax.dot_general(tab_ref[1], block, dims, preferred_element_type=jnp.float32)
        for pair in range(group // 2):
            cut = slice(pair * LANES, (pair + 1) * LANES)
            re, im = real[:, cut], imag[:, cut]
            even = jnp.where(low, re, pltpu.roll(im, spectra, 1))
            odd = jnp.where(low, pltpu.roll(re, spectra, 1), im)
            row = step * group + 2 * pair
            t_ref[pl.ds(row, CHANNELS, stride=inputs), :] = even
            t_ref[pl.ds(row + 1, CHANNELS, stride=inputs), :] = odd
        return carry

    lax.fori_loop(0, inputs // group, dft, 0)

    chunk = 16

    def cast(step, carry):
        first = pl.multiple_of(step * chunk, chunk)
        rows = t_ref[pl.ds(first * inputs, chunk * inputs), :]
        o_ref[pl.ds(first, chunk)] = rows.astype(jnp.bfloat16).reshape(chunk, inputs, LANES)
        return carry

    lax.fori_loop(0, CHANNELS // chunk, cast, 0)


def channelize(voltages, earlier):
    inputs = voltages.shape[0]
    spectra = voltages.shape[1] // FFT_LEN
    vmem = pl.BlockSpec(memory_space=pltpu.VMEM)
    return pl.pallas_call(
        channelize_kernel,
        out_shape=jax.ShapeDtypeStruct((CHANNELS, inputs, 2 * spectra), jnp.bfloat16),
        in_specs=[vmem] * 4,
        out_specs=vmem,
        scratch_shapes=[
            pltpu.VMEM((FFT_LEN // LANES, inputs * spectra, LANES), jnp.float32),
            pltpu.VMEM((CHANNELS * inputs, 2 * spectra), jnp.float32),
        ],
        compiler_params=pltpu.CompilerParams(vmem_limit_bytes=32 << 20),
        name="channelize",
    )(voltages, earlier, window_table(TAPS, FFT_LEN), fourier_table(CHANNELS, FFT_LEN))


def correlate_kernel(groups, slots, scale, r_ref, o_ref, x_ref, y_ref):
    height = r_ref.shape[1]

    @pl.when(pl.program_id(0) == 0)
    def _():
        half = LANES // 2
        upper = lax.broadcasted_iota(jnp.int32, (height, LANES), 1) >= half

        def place(g, carry):
            rows = pl.ds(pl.multiple_of(g * height, height), height)
            for t in range(slots):
                lanes = slice(t * LANES, (t + 1) * LANES)
                value = r_ref[g * slots + t]
                turned = pltpu.roll(value.astype(jnp.float32), half, 1)
                x_ref[rows, lanes] = value
                y_ref[rows, lanes] = jnp.where(upper, -turned, turned).astype(jnp.bfloat16)
            return carry

        lax.fori_loop(0, groups, place, 0)

    row_block, col_block = o_ref.shape[2], o_ref.shape[3]
    col_count = x_ref.shape[0] // col_block
    row = pl.multiple_of((pl.program_id(0) // col_count) * row_block, row_block)
    col = pl.multiple_of((pl.program_id(0) % col_count) * col_block, col_block)
    right = x_ref[pl.ds(col, col_block), :]
    dims = (((1,), (1,)), ((), ()))
    for part, ref in enumerate((x_ref, y_ref)):
        left = ref[pl.ds(row, row_block), :]
        value = lax.dot_general(left, right, dims, preferred_element_type=jnp.float32)
        o_ref[0, part] = (value * scale).astype(jnp.bfloat16)


def correlate(received, groups, slots, row_count, col_count, scale):
    height = received.shape[1]
    total = groups * height
    row_block, col_block = total // row_count, total // col_count
    tiles = row_count * col_count
    return pl.pallas_call(
        functools.partial(correlate_kernel, groups, slots, scale),
        grid=(tiles,),
        out_shape=jax.ShapeDtypeStruct((tiles, 2, row_block, col_block), jnp.bfloat16),
        in_specs=[pl.BlockSpec(memory_space=pltpu.VMEM)],
        out_specs=pl.BlockSpec((1, 2, row_block, col_block), lambda i: (i, 0, 0, 0)),
        scratch_shapes=[pltpu.VMEM((total, slots * LANES), jnp.bfloat16)] * 2,
        compiler_params=pltpu.CompilerParams(vmem_limit_bytes=32 << 20),
        name="correlate",
    )(received)


def per_device(voltages):
    slot_spectra = voltages.shape[1] // FFT_LEN
    row_count = lax.axis_size("row")
    col_count = lax.axis_size("col")
    slots = row_count * col_count
    groups = lax.axis_size("chan")
    tail = voltages[:, (slot_spectra - TAPS + 1) * FFT_LEN :]
    earlier = lax.ppermute(tail, ("row", "col"), [(i, i + 1) for i in range(slots - 1)])
    spectra = channelize(voltages, earlier)
    turned = lax.all_to_all(spectra, ("chan", "row", "col"), split_axis=0, concat_axis=0, tiled=True)
    tiles = correlate(turned, groups, slots, row_count, col_count, 1.0 / (slot_spectra * slots))
    summed = lax.all_to_all(tiles, ("row", "col"), split_axis=0, concat_axis=0, tiled=True)
    return summed.astype(jnp.float32)


def solution(mesh):
    placed = (P("chan", ("row", "col")),)
    return jax.shard_map(
        per_device,
        mesh=mesh,
        in_specs=placed,
        out_specs=P("chan", None, "row", "col"),
        check_vma=False,
    )
```

```python
import functools

import jax
import jax.numpy as jnp
import ml_dtypes
import numpy as np
from jax import lax
from jax.experimental import pallas as pl
from jax.experimental.pallas import tpu as pltpu
from jax.sharding import PartitionSpec as P

FFT_LEN = 512
TAPS = 8
CHANNELS = 256
LANES = 128
CORES = 2
HEAD = 8
CHUNKS = FFT_LEN // LANES
ALL = ("chan", "row", "col")
VMEM = pl.BlockSpec(memory_space=pltpu.VMEM)
SMEM = pl.BlockSpec(memory_space=pltpu.SMEM)
NT = (((1,), (1,)), ((), ()))


def window_table(taps, length):
    count = taps * length
    position = np.arange(count, dtype=np.float64)
    offset = (position - count / 2 + 0.5) / length
    taper = 0.5 - 0.5 * np.cos(2.0 * np.pi * (position + 0.5) / count)
    values = np.sinc(offset) * taper
    values = values / np.sqrt(np.sum(values * values))
    return values.reshape(taps, length).astype(np.float32)


def fourier_table(channels, length):
    channel_index = np.arange(channels)[:, None]
    sample_index = np.arange(length)[None, :]
    phase = (channel_index * sample_index % length) * (2.0 * np.pi / length)
    return np.stack([np.cos(phase), -np.sin(phase)]).astype(np.float32).astype(ml_dtypes.bfloat16)


def chunk_channels(chunk, rows, cols):
    slots = rows * cols
    pairs = CHANNELS // (CORES * slots)
    found = []
    for pair in range(pairs):
        for row in range(rows):
            for col in range(cols):
                core = col if chunk == 0 else 1 - col
                found.append((pair * CORES + core) * slots + row * cols + col)
    return np.array(found)


def fir_rows(read, first, last, store, w_ref, rows, lane):
    height = rows.size
    taps = [jnp.broadcast_to(w_ref[t : t + 1, pl.ds(lane, LANES)], (height, LANES)) for t in range(TAPS)]
    sums = {}
    for block in range(first, last + TAPS - 1):
        value = read(block).astype(jnp.float32)
        for t in range(TAPS):
            s = block - t
            if first <= s < last:
                term = taps[t] * value
                sums[s] = term if t == 0 else sums[s] + term
        done = block - TAPS + 1
        if done >= first:
            store(done, sums.pop(done))


def for_tiles(inputs, body):
    row_tile = 16

    def step(index, carry):
        chunk = index % CHUNKS
        first_row = pl.multiple_of((index // CHUNKS) * row_tile, row_tile)
        body(pl.ds(first_row, row_tile), first_row, chunk, pl.multiple_of(chunk * LANES, LANES))
        return carry

    lax.fori_loop(0, (inputs // row_tile) * CHUNKS, step, 0)


def fir_kernel(v_ref, w_ref, f_ref):
    inputs = v_ref.shape[0]
    spectra = v_ref.shape[1] // FFT_LEN
    body_len = spectra - HEAD

    def tile(rows, first_row, chunk, lane):
        def read(block):
            return v_ref[rows, pl.ds((block - TAPS + 1) * FFT_LEN + lane, LANES)]

        def store(s, value):
            f_ref[chunk, pl.ds(first_row * body_len + s - HEAD, rows.size, stride=body_len), :] = value

        fir_rows(read, HEAD, spectra, store, w_ref, rows, lane)

    for_tiles(inputs, tile)


def dft(f_ref, head_ref, tab_ref, o_ref, t_ref):
    inputs = o_ref.shape[1] * CORES
    channels = tab_ref.shape[0] // 2
    body_len = f_ref.shape[1] // inputs
    spectra = body_len + HEAD
    group = 8
    low = lax.broadcasted_iota(jnp.int32, (channels, LANES), 1) < spectra

    def transform(step, carry):
        columns = []
        for c in range(CHUNKS):
            parts = []
            for j in range(group):
                i = step * group + j
                parts.append(head_ref[c, pl.ds(pl.multiple_of(i * HEAD, HEAD), HEAD), :])
                parts.append(f_ref[c, pl.ds(pl.multiple_of(i * body_len, 8), body_len), :])
            columns.append(jnp.concatenate(parts, axis=0).astype(jnp.bfloat16))
        block = jnp.concatenate(columns, axis=1)
        both = lax.dot_general(tab_ref[...], block, NT, preferred_element_type=jnp.float32)
        for pair in range(group // 2):
            cut = slice(pair * LANES, (pair + 1) * LANES)
            re, im = both[:channels, cut], both[channels:, cut]
            even = jnp.where(low, re, pltpu.roll(im, spectra, 1))
            odd = jnp.where(low, pltpu.roll(re, spectra, 1), im)
            row = step * group + 2 * pair
            t_ref[pl.ds(row, channels, stride=inputs), :] = even
            t_ref[pl.ds(row + 1, channels, stride=inputs), :] = odd
        return carry

    lax.fori_loop(0, inputs // group, transform, 0)

    half = inputs // CORES
    slots = 8

    def cast(pair, carry):
        for core in range(CORES):
            for slot in range(slots):
                first = pl.multiple_of((pair * slots + slot) * inputs + core * half, half)
                rows = t_ref[pl.ds(first, half), :]
                o_ref[pair * (CORES * slots) + core * slots + slot] = rows.astype(jnp.bfloat16)
        return carry

    lax.fori_loop(0, channels // slots, cast, 0)


def head_kernel(v_ref, h_ref, f_ref, w_ref, tab_ref, o_ref, head_ref, t_ref):
    def tile(rows, first_row, chunk, lane):
        def read(block):
            if block < TAPS - 1:
                return h_ref[rows, pl.ds(block * FFT_LEN + lane, LANES)]
            return v_ref[rows, pl.ds((block - TAPS + 1) * FFT_LEN + lane, LANES)]

        def store(s, value):
            head_ref[chunk, pl.ds(first_row * HEAD + s, rows.size, stride=HEAD), :] = value

        fir_rows(read, 0, HEAD, store, w_ref, rows, lane)

    for_tiles(v_ref.shape[0], tile)
    dft(f_ref, head_ref, tab_ref, o_ref, t_ref)


def params(mib=24):
    return pltpu.CompilerParams(vmem_limit_bytes=mib << 20)


def cost(flops, nbytes):
    return pl.CostEstimate(flops=flops, bytes_accessed=nbytes, transcendentals=0)


def channelize(voltages, earlier, rows, cols):
    inputs = voltages.shape[0]
    spectra = voltages.shape[1] // FFT_LEN
    window = window_table(TAPS, FFT_LEN)
    table = fourier_table(CHANNELS, FFT_LEN)
    tables = [table[:, chunk_channels(c, rows, cols)].reshape(-1, FFT_LEN) for c in range(2)]
    channels = CHANNELS // 2
    body = pl.pallas_call(
        fir_kernel,
        out_shape=jax.ShapeDtypeStruct((CHUNKS, inputs * (spectra - HEAD), LANES), jnp.float32),
        in_specs=[VMEM] * 2,
        out_specs=VMEM,
        compiler_params=params(),
        cost_estimate=cost(16 * voltages.size, 6 * voltages.size),
        name="fir",
    )(voltages, window)
    message = jax.ShapeDtypeStruct((CHANNELS, inputs // CORES, 2 * spectra), jnp.bfloat16)
    scratch = [pltpu.VMEM((channels * inputs, 2 * spectra), jnp.float32)]
    work = cost(4 * channels * FFT_LEN * inputs * spectra, 6 * voltages.size)
    first, head = pl.pallas_call(
        head_kernel,
        out_shape=[message, jax.ShapeDtypeStruct((CHUNKS, inputs * HEAD, LANES), jnp.float32)],
        in_specs=[VMEM] * 5,
        out_specs=[VMEM] * 2,
        scratch_shapes=scratch,
        compiler_params=params(),
        cost_estimate=work,
        name="head_dft",
    )(voltages[:, : HEAD * FFT_LEN], earlier, body, window, tables[0])
    second = pl.pallas_call(
        dft,
        out_shape=message,
        in_specs=[VMEM] * 3,
        out_specs=VMEM,
        scratch_shapes=scratch,
        compiler_params=params(),
        cost_estimate=work,
        name="dft",
    )(body, head, tables[1])
    return first, second


def correlate_kernel(groups, rows, cols, scale, at_ref, mine_ref, other_ref, *refs):
    outs, (x_ref, y_ref) = refs[:-2], refs[-2:]
    core, row = at_ref[0], at_ref[1]
    part = mine_ref.shape[1]
    height = CORES * part
    slots = rows * cols
    half = LANES // 2

    def place(g, carry):
        for ref, owner in ((mine_ref, core), (other_ref, 1 - core)):
            dest = pl.ds(pl.multiple_of(g * height + owner * part, part), part)
            for t in range(slots):
                x_ref[dest, t * LANES : (t + 1) * LANES] = ref[g * slots + t]
        return carry

    lax.fori_loop(0, groups, place, 0)

    row_block = groups * height // rows
    row_half = row_block // CORES
    col_block = groups * height // cols
    upper = lax.broadcasted_iota(jnp.int32, (row_half, LANES), 1) >= half
    for dy in range(rows):
        first = pl.multiple_of(lax.rem(row + dy, rows) * row_block + core * row_half, row_half)
        left = pl.ds(first, row_half)
        for t in range(slots):
            lanes = slice(t * LANES, (t + 1) * LANES)
            turned = pltpu.roll(x_ref[left, lanes].astype(jnp.float32), half, 1)
            y_ref[:, lanes] = jnp.where(upper, -turned, turned).astype(jnp.bfloat16)
        for d in range(cols):
            col = jnp.bitwise_xor(core, d)
            right = x_ref[pl.ds(pl.multiple_of(col * col_block, col_block), col_block), :]
            real = lax.dot_general(x_ref[left, :], right, NT, preferred_element_type=jnp.float32)
            imag = lax.dot_general(y_ref[...], right, NT, preferred_element_type=jnp.float32)
            out = outs[dy * cols + d]
            out[0] = (real * scale).astype(jnp.bfloat16)
            out[1] = (imag * scale).astype(jnp.bfloat16)


def correlate(at, mine, other, groups, rows, cols, scale):
    total = groups * mine.shape[1] * CORES
    depth = rows * cols * LANES
    row_half, col_block = total // rows // CORES, total // cols
    piece = jax.ShapeDtypeStruct((2, row_half, col_block), jnp.bfloat16)
    return pl.pallas_call(
        functools.partial(correlate_kernel, groups, rows, cols, scale),
        out_shape=[piece] * (rows * cols),
        in_specs=[SMEM, VMEM, VMEM],
        out_specs=[VMEM] * (rows * cols),
        scratch_shapes=[pltpu.VMEM((total, depth), jnp.bfloat16), pltpu.VMEM((row_half, depth), jnp.bfloat16)],
        compiler_params=params(),
        cost_estimate=cost(2 * total * total * depth, 8 * total * depth),
        name="correlate",
    )(at, mine, other)


def widen_kernel(count, aliased, where_ref, *refs):
    o_ref = refs[-1]
    for j in range(count):

        @pl.when(pl.program_id(0) == j)
        def _():
            o_ref[0] = refs[aliased + j][...].astype(jnp.float32)


def widen(pieces, where, shape, into=None):
    _, row_half, col_block = pieces[0].shape
    aliased = 0 if into is None else 1
    spec = pltpu.PrefetchScalarGridSpec(
        num_scalar_prefetch=1,
        grid=(len(pieces),),
        in_specs=[pl.BlockSpec(memory_space=pl.ANY)] * aliased + [VMEM] * len(pieces),
        out_specs=pl.BlockSpec((1, 2, row_half, col_block), lambda j, at: (at[0, j], 0, at[1, j], 0)),
    )
    return pl.pallas_call(
        functools.partial(widen_kernel, len(pieces), aliased),
        grid_spec=spec,
        out_shape=jax.ShapeDtypeStruct(shape, jnp.float32),
        input_output_aliases={1: 0} if aliased else {},
        compiler_params=params(),
        cost_estimate=cost(len(pieces) * pieces[0].size, 6 * len(pieces) * pieces[0].size),
        name="widen",
    )(where, *([] if into is None else [into]), *pieces)


def per_device(voltages):
    slot_spectra = voltages.shape[1] // FFT_LEN
    rows = lax.axis_size("row")
    cols = lax.axis_size("col")
    slots = rows * cols
    groups = lax.axis_size("chan")
    tail = voltages[:, (slot_spectra - TAPS + 1) * FFT_LEN :]
    earlier = lax.ppermute(tail, ("row", "col"), [(i, i + 1) for i in range(slots - 1)])
    core = lax.axis_index("chan") % CORES
    row, col = lax.axis_index("row"), lax.axis_index("col")
    at = jnp.stack([core, row]).astype(jnp.int32)
    scale = 1.0 / (slot_spectra * slots)
    total = groups * voltages.shape[0]
    shape = (slots, 2, total // rows, total // cols)
    messages = channelize(voltages, earlier, rows, cols)
    swap = [(i, i ^ 1) for i in range(groups)]
    arrived = [lax.all_to_all(message, ALL, split_axis=0, concat_axis=0, tiled=True) for message in messages]
    out = None
    for chunk, mine in enumerate(arrived):
        if chunk:
            mine, got = lax.optimization_barrier((mine, got))
            out = widen(got, where, shape)
        other = lax.ppermute(mine, "chan", swap)
        sent = correlate(at, mine, other, groups, rows, cols, scale)
        got, channel, half = [], [], []
        for dy in range(rows):
            for d in range(cols):
                pairs = []
                for c in range(groups):
                    for r in range(rows):
                        for x in range(cols):
                            to_core = x if chunk == 0 else 1 - x
                            target = (c - c % CORES + to_core, (r + dy) % rows, (c % CORES) ^ d)
                            pairs.append(((c * rows + r) * cols + x, (target[0] * rows + target[1]) * cols + target[2]))
                got.append(lax.ppermute(sent[dy * cols + d], ALL, pairs))
                from_col = core if chunk == 0 else 1 - core
                channel.append((row + rows - dy) % rows * cols + from_col)
                half.append(jnp.bitwise_xor(col, d))
        where = jnp.stack([jnp.stack(channel), jnp.stack(half)]).astype(jnp.int32)
    return widen(got, where, shape, out)


def solution(mesh):
    placed = (P("chan", ("row", "col")),)
    return jax.shard_map(
        per_device,
        mesh=mesh,
        in_specs=placed,
        out_specs=P("chan", None, "row", "col"),
        check_vma=False,
    )
```

```python
import functools

import jax
import jax.numpy as jnp
import ml_dtypes
import numpy as np
from jax import lax
from jax.experimental import pallas as pl
from jax.experimental.pallas import tpu as pltpu
from jax.sharding import Mesh
from jax.sharding import PartitionSpec as P

FFT_LEN = 512
TAPS = 8
CHANNELS = 256
LANES = 128
CORES = 2
HEAD = 8
CHUNKS = FFT_LEN // LANES
CHIPS = ("pair", "row", "col")
ALL = ("pair", "core", "row", "col")
VMEM = pl.BlockSpec(memory_space=pltpu.VMEM)
SMEM = pl.BlockSpec(memory_space=pltpu.SMEM)
NT = (((1,), (1,)), ((), ()))


def window_table(taps, length):
    count = taps * length
    position = np.arange(count, dtype=np.float64)
    offset = (position - count / 2 + 0.5) / length
    taper = 0.5 - 0.5 * np.cos(2.0 * np.pi * (position + 0.5) / count)
    values = np.sinc(offset) * taper
    values = values / np.sqrt(np.sum(values * values))
    return values.reshape(taps, length).astype(np.float32)


def fourier_table(channels, length):
    channel_index = np.arange(channels)[:, None]
    sample_index = np.arange(length)[None, :]
    phase = (channel_index * sample_index % length) * (2.0 * np.pi / length)
    return np.stack([np.cos(phase), -np.sin(phase)]).astype(np.float32).astype(ml_dtypes.bfloat16)


def chunk_channels(chunk, rows, cols):
    slots = rows * cols
    pairs = CHANNELS // (CORES * slots)
    found = []
    for pair in range(pairs):
        for row in range(rows):
            for col in range(cols):
                core = col if chunk == 0 else 1 - col
                found.append((pair * CORES + core) * slots + row * cols + col)
    return np.array(found)


def fir_rows(read, first, last, store, w_ref, rows, lane):
    height = rows.size
    taps = [jnp.broadcast_to(w_ref[t : t + 1, pl.ds(lane, LANES)], (height, LANES)) for t in range(TAPS)]
    sums = {}
    for block in range(first, last + TAPS - 1):
        value = read(block).astype(jnp.float32)
        for t in range(TAPS):
            s = block - t
            if first <= s < last:
                term = taps[t] * value
                sums[s] = term if t == 0 else sums[s] + term
        done = block - TAPS + 1
        if done >= first:
            store(done, sums.pop(done))


def for_tiles(inputs, body):
    row_tile = 16

    def step(index, carry):
        chunk = index % CHUNKS
        first_row = pl.multiple_of((index // CHUNKS) * row_tile, row_tile)
        body(pl.ds(first_row, row_tile), first_row, chunk, pl.multiple_of(chunk * LANES, LANES))
        return carry

    lax.fori_loop(0, (inputs // row_tile) * CHUNKS, step, 0)


def fir_kernel(v_ref, w_ref, f_ref):
    inputs = v_ref.shape[0]
    spectra = v_ref.shape[1] // FFT_LEN
    body_len = spectra - HEAD

    def tile(rows, first_row, chunk, lane):
        def read(block):
            return v_ref[rows, pl.ds((block - TAPS + 1) * FFT_LEN + lane, LANES)]

        def store(s, value):
            f_ref[chunk, pl.ds(first_row * body_len + s - HEAD, rows.size, stride=body_len), :] = value

        fir_rows(read, HEAD, spectra, store, w_ref, rows, lane)

    for_tiles(inputs, tile)


def dft(f_ref, head_ref, tab_ref, o_ref, t_ref):
    inputs = o_ref.shape[1]
    channels = tab_ref.shape[0] // 2
    body_len = f_ref.shape[1] // inputs
    spectra = body_len + HEAD
    group = 8
    low = lax.broadcasted_iota(jnp.int32, (channels, LANES), 1) < spectra

    def transform(step, carry):
        columns = []
        for c in range(CHUNKS):
            parts = []
            for j in range(group):
                i = step * group + j
                parts.append(head_ref[c, pl.ds(pl.multiple_of(i * HEAD, HEAD), HEAD), :])
                parts.append(f_ref[c, pl.ds(pl.multiple_of(i * body_len, 8), body_len), :])
            columns.append(jnp.concatenate(parts, axis=0).astype(jnp.bfloat16))
        block = jnp.concatenate(columns, axis=1)
        both = lax.dot_general(tab_ref[...], block, NT, preferred_element_type=jnp.float32)
        for pair in range(group // 2):
            cut = slice(pair * LANES, (pair + 1) * LANES)
            re, im = both[:channels, cut], both[channels:, cut]
            even = jnp.where(low, re, pltpu.roll(im, spectra, 1))
            odd = jnp.where(low, pltpu.roll(re, spectra, 1), im)
            row = step * group + 2 * pair
            t_ref[pl.ds(row, channels, stride=inputs), :] = even
            t_ref[pl.ds(row + 1, channels, stride=inputs), :] = odd
        return carry

    lax.fori_loop(0, inputs // group, transform, 0)

    step = 8

    def cast(index, carry):
        for j in range(step):
            first = pl.multiple_of((index * step + j) * inputs, inputs)
            o_ref[index * step + j] = t_ref[pl.ds(first, inputs), :].astype(jnp.bfloat16)
        return carry

    lax.fori_loop(0, channels // step, cast, 0)


def head_kernel(v_ref, h_ref, f_ref, w_ref, tab_ref, o_ref, head_ref, t_ref):
    def tile(rows, first_row, chunk, lane):
        def read(block):
            if block < TAPS - 1:
                return h_ref[rows, pl.ds(block * FFT_LEN + lane, LANES)]
            return v_ref[rows, pl.ds((block - TAPS + 1) * FFT_LEN + lane, LANES)]

        def store(s, value):
            head_ref[chunk, pl.ds(first_row * HEAD + s, rows.size, stride=HEAD), :] = value

        fir_rows(read, 0, HEAD, store, w_ref, rows, lane)

    for_tiles(v_ref.shape[0], tile)
    dft(f_ref, head_ref, tab_ref, o_ref, t_ref)


def params(mib=12):
    return pltpu.CompilerParams(vmem_limit_bytes=mib << 20)


def cost(flops, nbytes):
    return pl.CostEstimate(flops=flops, bytes_accessed=nbytes, transcendentals=0)


def channelize(voltages, earlier, rows, cols):
    inputs = voltages.shape[0]
    spectra = voltages.shape[1] // FFT_LEN
    window = window_table(TAPS, FFT_LEN)
    table = fourier_table(CHANNELS, FFT_LEN)
    tables = [table[:, chunk_channels(c, rows, cols)].reshape(-1, FFT_LEN) for c in range(2)]
    channels = CHANNELS // 2
    body = pl.pallas_call(
        fir_kernel,
        out_shape=jax.ShapeDtypeStruct((CHUNKS, inputs * (spectra - HEAD), LANES), jnp.float32),
        in_specs=[VMEM] * 2,
        out_specs=VMEM,
        compiler_params=params(),
        cost_estimate=cost(16 * voltages.size, 6 * voltages.size),
        name="fir",
    )(voltages, window)
    message = jax.ShapeDtypeStruct((channels, inputs, 2 * spectra), jnp.bfloat16)
    scratch = [pltpu.VMEM((channels * inputs, 2 * spectra), jnp.float32)]
    work = cost(4 * channels * FFT_LEN * inputs * spectra, 6 * voltages.size)
    first, head = pl.pallas_call(
        head_kernel,
        out_shape=[message, jax.ShapeDtypeStruct((CHUNKS, inputs * HEAD, LANES), jnp.float32)],
        in_specs=[VMEM] * 5,
        out_specs=[VMEM] * 2,
        scratch_shapes=scratch,
        compiler_params=params(),
        cost_estimate=work,
        name="head_dft",
    )(voltages[:, : HEAD * FFT_LEN], earlier, body, window, tables[0])
    second = pl.pallas_call(
        dft,
        out_shape=message,
        in_specs=[VMEM] * 3,
        out_specs=VMEM,
        scratch_shapes=scratch,
        compiler_params=params(),
        cost_estimate=work,
        name="dft",
    )(body, head, tables[1])
    return first, second


def correlate_kernel(pairs, rows, cols, scale, at_ref, mine_ref, other_ref, *refs):
    outs, (x_ref, l_ref) = refs[:-2], refs[-2:]
    core, row = at_ref[0], at_ref[1]
    height = mine_ref.shape[1]
    slots = rows * cols
    half = LANES // 2

    def place(pair, carry):
        for ref, owner in ((mine_ref, core), (other_ref, 1 - core)):
            dest = pl.ds(pl.multiple_of((pair * CORES + owner) * height, height), height)
            for t in range(slots):
                x_ref[dest, t * LANES : (t + 1) * LANES] = ref[pair * slots + t]
        return carry

    lax.fori_loop(0, pairs, place, 0)

    row_block = x_ref.shape[0] // rows
    part = row_block // CORES
    col_block = x_ref.shape[0] // cols
    upper = lax.broadcasted_iota(jnp.int32, (part, LANES), 1) >= half
    for dy in range(rows):
        first = pl.multiple_of(lax.rem(row + dy, rows) * row_block + core * part, part)
        left = pl.ds(first, part)
        for t in range(slots):
            lanes = slice(t * LANES, (t + 1) * LANES)
            value = x_ref[left, lanes]
            turned = pltpu.roll(value.astype(jnp.float32), half, 1)
            l_ref[2 * dy * part : (2 * dy + 1) * part, lanes] = value
            l_ref[(2 * dy + 1) * part : (2 * dy + 2) * part, lanes] = jnp.where(upper, -turned, turned).astype(jnp.bfloat16)
    joint = 2
    for d in range(cols):
        col = jnp.bitwise_xor(core, d)
        right = x_ref[pl.ds(pl.multiple_of(col * col_block, col_block), col_block), :]
        for dy in range(0, rows, joint):
            left = l_ref[2 * dy * part : 2 * (dy + joint) * part, :]
            value = lax.dot_general(left, right, NT, preferred_element_type=jnp.float32) * scale
            for j in range(joint):
                for p in range(2):
                    outs[(dy + j) * cols + d][p] = value[(2 * j + p) * part : (2 * j + p + 1) * part].astype(jnp.bfloat16)


def correlate(at, mine, other, pairs, rows, cols, scale):
    total = pairs * mine.shape[1] * CORES
    depth = rows * cols * LANES
    row_half, col_block = total // rows // CORES, total // cols
    piece = jax.ShapeDtypeStruct((2, row_half, col_block), jnp.bfloat16)
    return pl.pallas_call(
        functools.partial(correlate_kernel, pairs, rows, cols, scale),
        out_shape=[piece] * (rows * cols),
        in_specs=[SMEM, VMEM, VMEM],
        out_specs=[VMEM] * (rows * cols),
        scratch_shapes=[pltpu.VMEM((total, depth), jnp.bfloat16), pltpu.VMEM((2 * rows * row_half, depth), jnp.bfloat16)],
        compiler_params=params(),
        cost_estimate=cost(2 * total * total * depth, 8 * total * depth),
        name="correlate",
    )(at, mine, other)


def widen_kernel(count, where_ref, *refs):
    pieces, o_ref, wide_ref, sems = refs[-count - 3 : -3], refs[-3], refs[-2], refs[-1]
    height = pieces[0].shape[1]
    copies = []
    for j, piece in enumerate(pieces):
        wide_ref[j] = piece[...].astype(jnp.float32)
        rows = pl.ds(pl.multiple_of(where_ref[1, j] * height, height), height)
        copies.append(pltpu.make_async_copy(wide_ref.at[j], o_ref.at[where_ref[0, j], :, rows, :], sems.at[j]))
        copies[-1].start()
    for copy in copies:
        copy.wait()


def widen(pieces, where, shape, into=None):
    count, piece = len(pieces), pieces[0]
    before = [] if into is None else [into]
    anywhere = pl.BlockSpec(memory_space=pl.ANY)
    return pl.pallas_call(
        functools.partial(widen_kernel, count),
        in_specs=[SMEM] + [anywhere] * len(before) + [VMEM] * count,
        out_specs=anywhere,
        out_shape=jax.ShapeDtypeStruct(shape, jnp.float32),
        scratch_shapes=[pltpu.VMEM((count, *piece.shape), jnp.float32), pltpu.SemaphoreType.DMA((count,))],
        input_output_aliases={1: 0} if before else {},
        compiler_params=params(8),
        cost_estimate=cost(count * piece.size, 6 * count * piece.size),
        name="widen",
    )(where, *before, *pieces)


def per_device(voltages):
    slot_spectra = voltages.shape[1] // FFT_LEN
    rows = lax.axis_size("row")
    cols = lax.axis_size("col")
    slots = rows * cols
    pairs = lax.axis_size("pair")
    tail = voltages[:, (slot_spectra - TAPS + 1) * FFT_LEN :]
    earlier = lax.ppermute(tail, ("row", "col"), [(i, i + 1) for i in range(slots - 1)])
    core = lax.axis_index("core")
    row, col = lax.axis_index("row"), lax.axis_index("col")
    at = jnp.stack([core, row]).astype(jnp.int32)
    scale = 1.0 / (slot_spectra * slots)
    total = pairs * CORES * voltages.shape[0]
    shape = (slots, 2, total // rows, total // cols)
    messages = channelize(voltages, earlier, rows, cols)
    arrived = [lax.all_to_all(message, CHIPS, split_axis=0, concat_axis=0, tiled=True) for message in messages]
    out = None
    for chunk, mine in enumerate(arrived):
        if chunk:
            mine, got = lax.optimization_barrier((mine, got))
            out = widen(got, where, shape)
        other = lax.ppermute(mine, "core", [(0, 1), (1, 0)])
        sent = correlate(at, mine, other, pairs, rows, cols, scale)
        got, channel, half = [], [], []
        for dy in range(rows):
            for d in range(cols):
                links = []
                for c in range(pairs * CORES):
                    for r in range(rows):
                        for x in range(cols):
                            to_core = x if chunk == 0 else 1 - x
                            target = (c - c % CORES + to_core, (r + dy) % rows, (c % CORES) ^ d)
                            links.append(((c * rows + r) * cols + x, (target[0] * rows + target[1]) * cols + target[2]))
                got.append(lax.ppermute(sent[dy * cols + d], ALL, links))
                from_col = core if chunk == 0 else 1 - core
                channel.append((row + rows - dy) % rows * cols + from_col)
                half.append(jnp.bitwise_xor(col, d))
        where = jnp.stack([jnp.stack(channel), jnp.stack(half)]).astype(jnp.int32)
    return widen(got, where, shape, out)


def solution(mesh):
    groups, rows, cols = mesh.devices.shape
    finer = Mesh(mesh.devices.reshape(groups // CORES, CORES, rows, cols), ALL)
    return jax.shard_map(
        per_device,
        mesh=finer,
        in_specs=(P(("pair", "core"), ("row", "col")),),
        out_specs=P(("pair", "core"), None, "row", "col"),
        check_vma=False,
    )
```

```python
import functools

import jax
import jax.numpy as jnp
import ml_dtypes
import numpy as np
from jax import lax
from jax.experimental import pallas as pl
from jax.experimental.pallas import tpu as pltpu
from jax.sharding import PartitionSpec as P

FFT_LEN = 512
TAPS = 8
CHANNELS = 256
LANES = 128
HEAD = 8
CHUNKS = FFT_LEN // LANES
ALL = ("chan", "row", "col")
VMEM = pl.BlockSpec(memory_space=pltpu.VMEM)
SMEM = pl.BlockSpec(memory_space=pltpu.SMEM)
NT = (((1,), (1,)), ((), ()))


def window_table(taps, length):
    count = taps * length
    position = np.arange(count, dtype=np.float64)
    offset = (position - count / 2 + 0.5) / length
    taper = 0.5 - 0.5 * np.cos(2.0 * np.pi * (position + 0.5) / count)
    values = np.sinc(offset) * taper
    values = values / np.sqrt(np.sum(values * values))
    return values.reshape(taps, length).astype(np.float32)


def fourier_table(channels, length):
    channel_index = np.arange(channels)[:, None]
    sample_index = np.arange(length)[None, :]
    phase = (channel_index * sample_index % length) * (2.0 * np.pi / length)
    return np.stack([np.cos(phase), -np.sin(phase)]).astype(np.float32).astype(ml_dtypes.bfloat16)


def fir_rows(read, first, last, store, w_ref, rows, lane):
    height = rows.size
    taps = [jnp.broadcast_to(w_ref[t : t + 1, pl.ds(lane, LANES)], (height, LANES)) for t in range(TAPS)]
    sums = {}
    for block in range(first, last + TAPS - 1):
        value = read(block).astype(jnp.float32)
        for t in range(TAPS):
            s = block - t
            if first <= s < last:
                term = taps[t] * value
                sums[s] = term if t == 0 else sums[s] + term
        done = block - TAPS + 1
        if done >= first:
            store(done, sums.pop(done))


def for_tiles(inputs, body):
    row_tile = 16

    def step(index, carry):
        chunk = index % CHUNKS
        first_row = pl.multiple_of((index // CHUNKS) * row_tile, row_tile)
        body(pl.ds(first_row, row_tile), first_row, chunk, pl.multiple_of(chunk * LANES, LANES))
        return carry

    lax.fori_loop(0, (inputs // row_tile) * CHUNKS, step, 0)


def fir_kernel(v_ref, w_ref, f_ref):
    inputs = v_ref.shape[0]
    spectra = v_ref.shape[1] // FFT_LEN
    body_len = spectra - HEAD

    def tile(rows, first_row, chunk, lane):
        def read(block):
            return v_ref[rows, pl.ds((block - TAPS + 1) * FFT_LEN + lane, LANES)]

        def store(s, value):
            f_ref[chunk, pl.ds(first_row * body_len + s - HEAD, rows.size, stride=body_len), :] = value

        fir_rows(read, HEAD, spectra, store, w_ref, rows, lane)

    for_tiles(inputs, tile)


def dft(f_ref, head_ref, tab_ref, o_ref, t_ref):
    inputs = o_ref.shape[1]
    channels = tab_ref.shape[0] // 2
    body_len = f_ref.shape[1] // inputs
    spectra = body_len + HEAD
    group = 8
    low = lax.broadcasted_iota(jnp.int32, (channels, LANES), 1) < spectra

    def transform(step, carry):
        columns = []
        for c in range(CHUNKS):
            parts = []
            for j in range(group):
                i = step * group + j
                parts.append(head_ref[c, pl.ds(pl.multiple_of(i * HEAD, HEAD), HEAD), :])
                parts.append(f_ref[c, pl.ds(pl.multiple_of(i * body_len, 8), body_len), :])
            columns.append(jnp.concatenate(parts, axis=0).astype(jnp.bfloat16))
        block = jnp.concatenate(columns, axis=1)
        both = lax.dot_general(tab_ref[...], block, NT, preferred_element_type=jnp.float32)
        for pair in range(group // 2):
            cut = slice(pair * LANES, (pair + 1) * LANES)
            re, im = both[:channels, cut], both[channels:, cut]
            even = jnp.where(low, re, pltpu.roll(im, spectra, 1))
            odd = jnp.where(low, pltpu.roll(re, spectra, 1), im)
            row = step * group + 2 * pair
            t_ref[pl.ds(row, channels, stride=inputs), :] = even
            t_ref[pl.ds(row + 1, channels, stride=inputs), :] = odd
        return carry

    lax.fori_loop(0, inputs // group, transform, 0)

    step = 8

    def cast(index, carry):
        for j in range(step):
            first = pl.multiple_of((index * step + j) * inputs, inputs)
            o_ref[index * step + j] = t_ref[pl.ds(first, inputs), :].astype(jnp.bfloat16)
        return carry

    lax.fori_loop(0, channels // step, cast, 0)


def head_kernel(v_ref, h_ref, f_ref, w_ref, tab_ref, o_ref, head_ref, t_ref):
    def tile(rows, first_row, chunk, lane):
        def read(block):
            if block < TAPS - 1:
                return h_ref[rows, pl.ds(block * FFT_LEN + lane, LANES)]
            return v_ref[rows, pl.ds((block - TAPS + 1) * FFT_LEN + lane, LANES)]

        def store(s, value):
            head_ref[chunk, pl.ds(first_row * HEAD + s, rows.size, stride=HEAD), :] = value

        fir_rows(read, 0, HEAD, store, w_ref, rows, lane)

    for_tiles(v_ref.shape[0], tile)
    dft(f_ref, head_ref, tab_ref, o_ref, t_ref)


def params(mib=12):
    return pltpu.CompilerParams(vmem_limit_bytes=mib << 20)


def cost(flops, nbytes):
    return pl.CostEstimate(flops=flops, bytes_accessed=nbytes, transcendentals=0)


def channelize(voltages, earlier):
    inputs = voltages.shape[0]
    spectra = voltages.shape[1] // FFT_LEN
    window = window_table(TAPS, FFT_LEN)
    table = fourier_table(CHANNELS, FFT_LEN).reshape(-1, FFT_LEN)
    body = pl.pallas_call(
        fir_kernel,
        out_shape=jax.ShapeDtypeStruct((CHUNKS, inputs * (spectra - HEAD), LANES), jnp.float32),
        in_specs=[VMEM] * 2,
        out_specs=VMEM,
        compiler_params=params(),
        cost_estimate=cost(16 * voltages.size, 6 * voltages.size),
        name="fir",
    )(voltages, window)
    return pl.pallas_call(
        head_kernel,
        out_shape=jax.ShapeDtypeStruct((CHANNELS, inputs, 2 * spectra), jnp.bfloat16),
        in_specs=[VMEM] * 5,
        out_specs=VMEM,
        scratch_shapes=[
            pltpu.VMEM((CHUNKS, inputs * HEAD, LANES), jnp.float32),
            pltpu.VMEM((CHANNELS * inputs, 2 * spectra), jnp.float32),
        ],
        compiler_params=params(),
        cost_estimate=cost(4 * CHANNELS * FFT_LEN * inputs * spectra, 6 * voltages.size),
        name="head_dft",
    )(voltages[:, : HEAD * FFT_LEN], earlier, body, window, table)


def correlate_kernel(groups, rows, cols, shifts, scale, at_ref, got_ref, *refs):
    outs, (x_ref, l_ref) = refs[:-2], refs[-2:]
    row, col = at_ref[0], at_ref[1]
    height = got_ref.shape[1]
    slots = rows * cols
    half = LANES // 2

    def place(g, carry):
        dest = pl.ds(pl.multiple_of(g * height, height), height)
        for t in range(slots):
            x_ref[dest, t * LANES : (t + 1) * LANES] = got_ref[g * slots + t]
        return carry

    lax.fori_loop(0, groups, place, 0)

    row_block = x_ref.shape[0] // rows
    col_block = x_ref.shape[0] // cols
    upper = lax.broadcasted_iota(jnp.int32, (row_block, LANES), 1) >= half
    for n, dy in enumerate(shifts):
        first = pl.multiple_of(lax.rem(row + dy, rows) * row_block, row_block)
        for t in range(slots):
            lanes = slice(t * LANES, (t + 1) * LANES)
            value = x_ref[pl.ds(first, row_block), lanes]
            turned = pltpu.roll(value.astype(jnp.float32), half, 1)
            l_ref[:row_block, lanes] = value
            l_ref[row_block:, lanes] = jnp.where(upper, -turned, turned).astype(jnp.bfloat16)
        for d in range(cols):
            block = pl.multiple_of(lax.rem(col + d, cols) * col_block, col_block)
            right = x_ref[pl.ds(block, col_block), :]
            value = lax.dot_general(l_ref[...], right, NT, preferred_element_type=jnp.float32) * scale
            for p in range(2):
                outs[n * cols + d][p] = value[p * row_block : (p + 1) * row_block].astype(jnp.bfloat16)


def correlate(at, got, groups, rows, cols, shifts, scale):
    total = groups * got.shape[1]
    depth = rows * cols * LANES
    row_block, col_block = total // rows, total // cols
    piece = jax.ShapeDtypeStruct((2, row_block, col_block), jnp.bfloat16)
    count = len(shifts) * cols
    return pl.pallas_call(
        functools.partial(correlate_kernel, groups, rows, cols, shifts, scale),
        out_shape=[piece] * count,
        in_specs=[SMEM, VMEM],
        out_specs=[VMEM] * count,
        scratch_shapes=[pltpu.VMEM((total, depth), jnp.bfloat16), pltpu.VMEM((2 * row_block, depth), jnp.bfloat16)],
        compiler_params=params(),
        cost_estimate=cost(4 * count * row_block * col_block * depth, 2 * total * depth + 2 * count * piece.size),
        name="correlate",
    )(at, got)


def widen_kernel(count, where_ref, *refs):
    pieces, o_ref, wide_ref, sems = refs[-count - 3 : -3], refs[-3], refs[-2], refs[-1]
    copies = []
    for j, piece in enumerate(pieces):
        wide_ref[j] = piece[...].astype(jnp.float32)
        copies.append(pltpu.make_async_copy(wide_ref.at[j], o_ref.at[where_ref[j]], sems.at[j]))
        copies[-1].start()
    for copy in copies:
        copy.wait()


def widen(pieces, where, shape, into=None):
    count, piece = len(pieces), pieces[0]
    before = [] if into is None else [into]
    anywhere = pl.BlockSpec(memory_space=pl.ANY)
    return pl.pallas_call(
        functools.partial(widen_kernel, count),
        in_specs=[SMEM] + [anywhere] * len(before) + [VMEM] * count,
        out_specs=anywhere,
        out_shape=jax.ShapeDtypeStruct(shape, jnp.float32),
        scratch_shapes=[pltpu.VMEM((count, *piece.shape), jnp.float32), pltpu.SemaphoreType.DMA((count,))],
        input_output_aliases={1: 0} if before else {},
        compiler_params=params(8),
        cost_estimate=cost(count * piece.size, 6 * count * piece.size),
        name="widen",
    )(where, *before, *pieces)


def per_device(voltages):
    slot_spectra = voltages.shape[1] // FFT_LEN
    rows = lax.axis_size("row")
    cols = lax.axis_size("col")
    slots = rows * cols
    groups = lax.axis_size("chan")
    tail = voltages[:, (slot_spectra - TAPS + 1) * FFT_LEN :]
    earlier = lax.ppermute(tail, ("row", "col"), [(i, i + 1) for i in range(slots - 1)])
    row, col = lax.axis_index("row"), lax.axis_index("col")
    at = jnp.stack([row, col]).astype(jnp.int32)
    scale = 1.0 / (slot_spectra * slots)
    total = groups * voltages.shape[0]
    shape = (slots, 2, total // rows, total // cols)
    message = channelize(voltages, earlier)
    turned = lax.all_to_all(message, ALL, split_axis=0, concat_axis=0, tiled=True)

    def travel(piece, dy, d):
        links = [(r * cols + c, (r + dy) % rows * cols + (c + d) % cols) for r in range(rows) for c in range(cols)]
        return piece if dy == d == 0 else lax.ppermute(piece, ("row", "col"), links)

    arrived = []
    for shifts in ((2,), (1, 3), (0,)):
        sent = correlate(at, turned, groups, rows, cols, shifts, scale)
        turned, sent = lax.optimization_barrier((turned, sent))
        for n, dy in enumerate(shifts):
            for d in range(cols):
                channel = (row + rows - dy) % rows * cols + (col + cols - d) % cols
                arrived.append((travel(sent[n * cols + d], dy, d), channel))
    out = None
    for batch in ((6, 0, 1), (2, 3), (4, 5, 7)):
        where = jnp.stack([arrived[b][1] for b in batch]).astype(jnp.int32)
        out = widen([arrived[b][0] for b in batch], where, shape, out)
    return out


def solution(mesh):
    return jax.shard_map(
        per_device,
        mesh=mesh,
        in_specs=(P("chan", ("row", "col")),),
        out_specs=P("chan", None, "row", "col"),
        check_vma=False,
    )
```

```python
import functools

import jax
import jax.numpy as jnp
import ml_dtypes
import numpy as np
from jax import lax
from jax.experimental import pallas as pl
from jax.experimental.pallas import tpu as pltpu
from jax.sharding import PartitionSpec as P

FFT_LEN = 512
TAPS = 8
CHANNELS = 256
LANES = 128
HEAD = 8
CHUNKS = FFT_LEN // LANES
ALL = ("chan", "row", "col")
VMEM = pl.BlockSpec(memory_space=pltpu.VMEM)
SMEM = pl.BlockSpec(memory_space=pltpu.SMEM)
NT = (((1,), (1,)), ((), ()))


def window_table(taps, length):
    count = taps * length
    position = np.arange(count, dtype=np.float64)
    offset = (position - count / 2 + 0.5) / length
    taper = 0.5 - 0.5 * np.cos(2.0 * np.pi * (position + 0.5) / count)
    values = np.sinc(offset) * taper
    values = values / np.sqrt(np.sum(values * values))
    return values.reshape(taps, length).astype(np.float32)


def fourier_table(channels, length):
    channel_index = np.arange(channels)[:, None]
    sample_index = np.arange(length)[None, :]
    phase = (channel_index * sample_index % length) * (2.0 * np.pi / length)
    return np.stack([np.cos(phase), -np.sin(phase)]).astype(np.float32).astype(ml_dtypes.bfloat16)


def fir_rows(read, first, last, store, w_ref, rows, lane):
    height = rows.size
    taps = [jnp.broadcast_to(w_ref[t : t + 1, pl.ds(lane, LANES)], (height, LANES)) for t in range(TAPS)]
    sums = {}
    for block in range(first, last + TAPS - 1):
        value = read(block).astype(jnp.float32)
        for t in range(TAPS):
            s = block - t
            if first <= s < last:
                term = taps[t] * value
                sums[s] = term if t == 0 else sums[s] + term
        done = block - TAPS + 1
        if done >= first:
            store(done, sums.pop(done))


def for_tiles(inputs, body):
    row_tile = 16

    def step(index, carry):
        chunk = index % CHUNKS
        first_row = pl.multiple_of((index // CHUNKS) * row_tile, row_tile)
        body(pl.ds(first_row, row_tile), first_row, chunk, pl.multiple_of(chunk * LANES, LANES))
        return carry

    lax.fori_loop(0, (inputs // row_tile) * CHUNKS, step, 0)


def fir_kernel(v_ref, w_ref, f_ref):
    inputs = v_ref.shape[0]
    spectra = v_ref.shape[1] // FFT_LEN
    body_len = spectra - HEAD

    def tile(rows, first_row, chunk, lane):
        def read(block):
            return v_ref[rows, pl.ds((block - TAPS + 1) * FFT_LEN + lane, LANES)]

        def store(s, value):
            f_ref[chunk, pl.ds(first_row * body_len + s - HEAD, rows.size, stride=body_len), :] = value

        fir_rows(read, HEAD, spectra, store, w_ref, rows, lane)

    for_tiles(inputs, tile)


def dft(f_ref, head_ref, tab_ref, o_ref, t_ref):
    inputs = o_ref.shape[1]
    channels = tab_ref.shape[0] // 2
    body_len = f_ref.shape[1] // inputs
    spectra = body_len + HEAD
    group = 8
    low = lax.broadcasted_iota(jnp.int32, (channels, LANES), 1) < spectra

    def transform(step, carry):
        columns = []
        for c in range(CHUNKS):
            parts = []
            for j in range(group):
                i = step * group + j
                parts.append(head_ref[c, pl.ds(pl.multiple_of(i * HEAD, HEAD), HEAD), :])
                parts.append(f_ref[c, pl.ds(pl.multiple_of(i * body_len, 8), body_len), :])
            columns.append(jnp.concatenate(parts, axis=0).astype(jnp.bfloat16))
        block = jnp.concatenate(columns, axis=1)
        both = lax.dot_general(tab_ref[...], block, NT, preferred_element_type=jnp.float32)
        for pair in range(group // 2):
            cut = slice(pair * LANES, (pair + 1) * LANES)
            re, im = both[:channels, cut], both[channels:, cut]
            even = jnp.where(low, re, pltpu.roll(im, spectra, 1))
            odd = jnp.where(low, pltpu.roll(re, spectra, 1), im)
            row = step * group + 2 * pair
            t_ref[pl.ds(row, channels, stride=inputs), :] = even
            t_ref[pl.ds(row + 1, channels, stride=inputs), :] = odd
        return carry

    lax.fori_loop(0, inputs // group, transform, 0)

    step = 8

    def cast(index, carry):
        for j in range(step):
            first = pl.multiple_of((index * step + j) * inputs, inputs)
            o_ref[index * step + j] = t_ref[pl.ds(first, inputs), :].astype(jnp.bfloat16)
        return carry

    lax.fori_loop(0, channels // step, cast, 0)


def head_kernel(v_ref, h_ref, f_ref, w_ref, tab_ref, o_ref, head_ref, t_ref):
    def tile(rows, first_row, chunk, lane):
        def read(block):
            if block < TAPS - 1:
                return h_ref[rows, pl.ds(block * FFT_LEN + lane, LANES)]
            return v_ref[rows, pl.ds((block - TAPS + 1) * FFT_LEN + lane, LANES)]

        def store(s, value):
            head_ref[chunk, pl.ds(first_row * HEAD + s, rows.size, stride=HEAD), :] = value

        fir_rows(read, 0, HEAD, store, w_ref, rows, lane)

    for_tiles(v_ref.shape[0], tile)
    dft(f_ref, head_ref, tab_ref, o_ref, t_ref)


def params(mib=12):
    return pltpu.CompilerParams(vmem_limit_bytes=mib << 20)


def cost(flops, nbytes):
    return pl.CostEstimate(flops=flops, bytes_accessed=nbytes, transcendentals=0)


def channelize(voltages, earlier):
    inputs = voltages.shape[0]
    spectra = voltages.shape[1] // FFT_LEN
    window = window_table(TAPS, FFT_LEN)
    table = fourier_table(CHANNELS, FFT_LEN).reshape(-1, FFT_LEN)
    body = pl.pallas_call(
        fir_kernel,
        out_shape=jax.ShapeDtypeStruct((CHUNKS, inputs * (spectra - HEAD), LANES), jnp.float32),
        in_specs=[VMEM] * 2,
        out_specs=VMEM,
        compiler_params=params(),
        cost_estimate=cost(16 * voltages.size, 6 * voltages.size),
        name="fir",
    )(voltages, window)
    return pl.pallas_call(
        head_kernel,
        out_shape=jax.ShapeDtypeStruct((CHANNELS, inputs, 2 * spectra), jnp.bfloat16),
        in_specs=[VMEM] * 5,
        out_specs=VMEM,
        scratch_shapes=[
            pltpu.VMEM((CHUNKS, inputs * HEAD, LANES), jnp.float32),
            pltpu.VMEM((CHANNELS * inputs, 2 * spectra), jnp.float32),
        ],
        compiler_params=params(),
        cost_estimate=cost(4 * CHANNELS * FFT_LEN * inputs * spectra, 6 * voltages.size),
        name="head_dft",
    )(voltages[:, : HEAD * FFT_LEN], earlier, body, window, table)


def correlate_kernel(groups, rows, cols, shifts, scale, at_ref, got_ref, *refs):
    outs, (x_ref, l_ref) = refs[:-2], refs[-2:]
    row, col = at_ref[0], at_ref[1]
    height = got_ref.shape[1]
    slots = rows * cols
    half = LANES // 2

    def place(g, carry):
        dest = pl.ds(pl.multiple_of(g * height, height), height)
        for t in range(slots):
            x_ref[dest, t * LANES : (t + 1) * LANES] = got_ref[g * slots + t]
        return carry

    lax.fori_loop(0, groups, place, 0)

    row_block = x_ref.shape[0] // rows
    col_block = x_ref.shape[0] // cols
    upper = lax.broadcasted_iota(jnp.int32, (row_block, LANES), 1) >= half
    for n, dy in enumerate(shifts):
        first = pl.multiple_of(lax.rem(row + dy, rows) * row_block, row_block)
        for t in range(slots):
            lanes = slice(t * LANES, (t + 1) * LANES)
            value = x_ref[pl.ds(first, row_block), lanes]
            turned = pltpu.roll(value.astype(jnp.float32), half, 1)
            l_ref[:row_block, lanes] = value
            l_ref[row_block:, lanes] = jnp.where(upper, -turned, turned).astype(jnp.bfloat16)
        for d in range(cols):
            block = pl.multiple_of(lax.rem(col + d, cols) * col_block, col_block)
            right = x_ref[pl.ds(block, col_block), :]
            value = lax.dot_general(l_ref[...], right, NT, preferred_element_type=jnp.float32) * scale
            for p in range(2):
                outs[n * cols + d][p] = value[p * row_block : (p + 1) * row_block].astype(jnp.bfloat16)


def correlate(at, got, groups, rows, cols, shifts, scale):
    total = groups * got.shape[1]
    depth = rows * cols * LANES
    row_block, col_block = total // rows, total // cols
    piece = jax.ShapeDtypeStruct((2, row_block, col_block), jnp.bfloat16)
    count = len(shifts) * cols
    return pl.pallas_call(
        functools.partial(correlate_kernel, groups, rows, cols, shifts, scale),
        out_shape=[piece] * count,
        in_specs=[SMEM, VMEM],
        out_specs=[VMEM] * count,
        scratch_shapes=[pltpu.VMEM((total, depth), jnp.bfloat16), pltpu.VMEM((2 * row_block, depth), jnp.bfloat16)],
        compiler_params=params(),
        cost_estimate=cost(4 * count * row_block * col_block * depth, 2 * total * depth + 2 * count * piece.size),
        name="correlate",
    )(at, got)


def widen_kernel(count, where_ref, *refs):
    pieces, (o_ref, narrow_ref, wide_ref, in_sems, out_sems) = refs[-count - 5 : -5], refs[-5:]
    reads = [pltpu.make_async_copy(piece, narrow_ref.at[j], in_sems.at[j]) for j, piece in enumerate(pieces)]
    for read in reads:
        read.start()
    writes = []
    for j, read in enumerate(reads):
        read.wait()
        wide_ref[j] = narrow_ref[j].astype(jnp.float32)
        writes.append(pltpu.make_async_copy(wide_ref.at[j], o_ref.at[where_ref[j]], out_sems.at[j]))
        writes[-1].start()
    for write in writes:
        write.wait()


def widen(pieces, where, shape, into=None):
    count, piece = len(pieces), pieces[0]
    before = [] if into is None else [into]
    anywhere = pl.BlockSpec(memory_space=pl.ANY)
    return pl.pallas_call(
        functools.partial(widen_kernel, count),
        in_specs=[SMEM] + [anywhere] * (len(before) + count),
        out_specs=anywhere,
        out_shape=jax.ShapeDtypeStruct(shape, jnp.float32),
        scratch_shapes=[
            pltpu.VMEM((count, *piece.shape), piece.dtype),
            pltpu.VMEM((count, *piece.shape), jnp.float32),
            pltpu.SemaphoreType.DMA((count,)),
            pltpu.SemaphoreType.DMA((count,)),
        ],
        input_output_aliases={1: 0} if before else {},
        compiler_params=params(8),
        cost_estimate=cost(count * piece.size, 6 * count * piece.size),
        name="widen",
    )(where, *before, *pieces)


def per_device(voltages):
    slot_spectra = voltages.shape[1] // FFT_LEN
    rows = lax.axis_size("row")
    cols = lax.axis_size("col")
    slots = rows * cols
    groups = lax.axis_size("chan")
    tail = voltages[:, (slot_spectra - TAPS + 1) * FFT_LEN :]
    earlier = lax.ppermute(tail, ("row", "col"), [(i, i + 1) for i in range(slots - 1)])
    row, col = lax.axis_index("row"), lax.axis_index("col")
    at = jnp.stack([row, col]).astype(jnp.int32)
    scale = 1.0 / (slot_spectra * slots)
    total = groups * voltages.shape[0]
    shape = (slots, 2, total // rows, total // cols)
    message = channelize(voltages, earlier)
    turned = lax.all_to_all(message, ALL, split_axis=0, concat_axis=0, tiled=True)

    def travel(piece, dy, d):
        links = [(r * cols + c, (r + dy) % rows * cols + (c + d) % cols) for r in range(rows) for c in range(cols)]
        return piece if dy == d == 0 else lax.ppermute(piece, ("row", "col"), links)

    arrived = []
    for shifts in ((1,), (3,), (0, 2)):
        sent = correlate(at, turned, groups, rows, cols, shifts, scale)
        turned, sent = lax.optimization_barrier((turned, sent))
        for n, dy in enumerate(shifts):
            for d in range(cols):
                channel = (row + rows - dy) % rows * cols + (col + cols - d) % cols
                arrived.append((travel(sent[n * cols + d], dy, d), channel))
    out = None
    for batch in ((0, 1, 4), (2, 3, 5), (6, 7)):
        where = jnp.stack([arrived[b][1] for b in batch]).astype(jnp.int32)
        out = widen([arrived[b][0] for b in batch], where, shape, out)
    return out


def solution(mesh):
    return jax.shard_map(
        per_device,
        mesh=mesh,
        in_specs=(P("chan", ("row", "col")),),
        out_specs=P("chan", None, "row", "col"),
        check_vma=False,
    )
```

```python
import functools

import jax
import jax.numpy as jnp
import ml_dtypes
import numpy as np
from jax import lax
from jax.experimental import pallas as pl
from jax.experimental.pallas import tpu as pltpu
from jax.sharding import PartitionSpec as P

FFT_LEN = 512
TAPS = 8
CHANNELS = 256
LANES = 128
HEAD = 8
CHUNKS = FFT_LEN // LANES
ALL = ("chan", "row", "col")
VMEM = pl.BlockSpec(memory_space=pltpu.VMEM)
SMEM = pl.BlockSpec(memory_space=pltpu.SMEM)
NT = (((1,), (1,)), ((), ()))


def window_table(taps, length):
    count = taps * length
    position = np.arange(count, dtype=np.float64)
    offset = (position - count / 2 + 0.5) / length
    taper = 0.5 - 0.5 * np.cos(2.0 * np.pi * (position + 0.5) / count)
    values = np.sinc(offset) * taper
    values = values / np.sqrt(np.sum(values * values))
    return values.reshape(taps, length).astype(np.float32)


def fourier_table(channels, length):
    channel_index = np.arange(channels)[:, None]
    sample_index = np.arange(length)[None, :]
    phase = (channel_index * sample_index % length) * (2.0 * np.pi / length)
    return np.stack([np.cos(phase), -np.sin(phase)]).astype(np.float32).astype(ml_dtypes.bfloat16)


def fir_rows(read, first, last, store, w_ref, rows, lane):
    height = rows.size
    taps = [jnp.broadcast_to(w_ref[t : t + 1, pl.ds(lane, LANES)], (height, LANES)) for t in range(TAPS)]
    sums = {}
    for block in range(first, last + TAPS - 1):
        value = read(block).astype(jnp.float32)
        for t in range(TAPS):
            s = block - t
            if first <= s < last:
                term = taps[t] * value
                sums[s] = term if t == 0 else sums[s] + term
        done = block - TAPS + 1
        if done >= first:
            store(done, sums.pop(done))


def for_tiles(inputs, body):
    row_tile = 16

    def step(index, carry):
        chunk = index % CHUNKS
        first_row = pl.multiple_of((index // CHUNKS) * row_tile, row_tile)
        body(pl.ds(first_row, row_tile), first_row, chunk, pl.multiple_of(chunk * LANES, LANES))
        return carry

    lax.fori_loop(0, (inputs // row_tile) * CHUNKS, step, 0)


def fir_kernel(v_ref, w_ref, f_ref):
    inputs = v_ref.shape[0]
    spectra = v_ref.shape[1] // FFT_LEN
    body_len = spectra - HEAD

    def tile(rows, first_row, chunk, lane):
        def read(block):
            return v_ref[rows, pl.ds((block - TAPS + 1) * FFT_LEN + lane, LANES)]

        def store(s, value):
            f_ref[chunk, pl.ds(first_row * body_len + s - HEAD, rows.size, stride=body_len), :] = value

        fir_rows(read, HEAD, spectra, store, w_ref, rows, lane)

    for_tiles(inputs, tile)


def dft(f_ref, head_ref, tab_ref, o_ref, t_ref):
    inputs = o_ref.shape[1]
    channels = tab_ref.shape[0] // 2
    body_len = f_ref.shape[1] // inputs
    spectra = body_len + HEAD
    group = 8
    low = lax.broadcasted_iota(jnp.int32, (channels, LANES), 1) < spectra

    def transform(step, carry):
        columns = []
        for c in range(CHUNKS):
            parts = []
            for j in range(group):
                i = step * group + j
                parts.append(head_ref[c, pl.ds(pl.multiple_of(i * HEAD, HEAD), HEAD), :])
                parts.append(f_ref[c, pl.ds(pl.multiple_of(i * body_len, 8), body_len), :])
            columns.append(jnp.concatenate(parts, axis=0).astype(jnp.bfloat16))
        block = jnp.concatenate(columns, axis=1)
        both = lax.dot_general(tab_ref[...], block, NT, preferred_element_type=jnp.float32)
        for pair in range(group // 2):
            cut = slice(pair * LANES, (pair + 1) * LANES)
            re, im = both[:channels, cut], both[channels:, cut]
            even = jnp.where(low, re, pltpu.roll(im, spectra, 1))
            odd = jnp.where(low, pltpu.roll(re, spectra, 1), im)
            row = step * group + 2 * pair
            t_ref[pl.ds(row, channels, stride=inputs), :] = even
            t_ref[pl.ds(row + 1, channels, stride=inputs), :] = odd
        return carry

    lax.fori_loop(0, inputs // group, transform, 0, unroll=True)

    step = 8

    def cast(index, carry):
        for j in range(step):
            first = pl.multiple_of((index * step + j) * inputs, inputs)
            o_ref[index * step + j] = t_ref[pl.ds(first, inputs), :].astype(jnp.bfloat16)
        return carry

    lax.fori_loop(0, channels // step, cast, 0, unroll=4)


def head_kernel(v_ref, h_ref, f_ref, w_ref, tab_ref, o_ref, head_ref, t_ref):
    def tile(rows, first_row, chunk, lane):
        def read(block):
            if block < TAPS - 1:
                return h_ref[rows, pl.ds(block * FFT_LEN + lane, LANES)]
            return v_ref[rows, pl.ds((block - TAPS + 1) * FFT_LEN + lane, LANES)]

        def store(s, value):
            head_ref[chunk, pl.ds(first_row * HEAD + s, rows.size, stride=HEAD), :] = value

        fir_rows(read, 0, HEAD, store, w_ref, rows, lane)

    for_tiles(v_ref.shape[0], tile)
    dft(f_ref, head_ref, tab_ref, o_ref, t_ref)


def params(mib=12):
    return pltpu.CompilerParams(vmem_limit_bytes=mib << 20)


def cost(flops, nbytes):
    return pl.CostEstimate(flops=flops, bytes_accessed=nbytes, transcendentals=0)


def channelize(voltages, earlier):
    inputs = voltages.shape[0]
    spectra = voltages.shape[1] // FFT_LEN
    window = window_table(TAPS, FFT_LEN)
    table = fourier_table(CHANNELS, FFT_LEN).reshape(-1, FFT_LEN)
    body = pl.pallas_call(
        fir_kernel,
        out_shape=jax.ShapeDtypeStruct((CHUNKS, inputs * (spectra - HEAD), LANES), jnp.float32),
        in_specs=[VMEM] * 2,
        out_specs=VMEM,
        compiler_params=params(),
        cost_estimate=cost(16 * voltages.size, 6 * voltages.size),
        name="fir",
    )(voltages, window)
    return pl.pallas_call(
        head_kernel,
        out_shape=jax.ShapeDtypeStruct((CHANNELS, inputs, 2 * spectra), jnp.bfloat16),
        in_specs=[VMEM] * 5,
        out_specs=VMEM,
        scratch_shapes=[
            pltpu.VMEM((CHUNKS, inputs * HEAD, LANES), jnp.float32),
            pltpu.VMEM((CHANNELS * inputs, 2 * spectra), jnp.float32),
        ],
        compiler_params=params(),
        cost_estimate=cost(4 * CHANNELS * FFT_LEN * inputs * spectra, 6 * voltages.size),
        name="head_dft",
    )(voltages[:, : HEAD * FFT_LEN], earlier, body, window, table)


def correlate_kernel(groups, rows, cols, shifts, scale, at_ref, got_ref, *refs):
    outs, (x_ref, l_ref) = refs[:-2], refs[-2:]
    row, col = at_ref[0], at_ref[1]
    height = got_ref.shape[1]
    slots = rows * cols
    half = LANES // 2

    def place(g, carry):
        dest = pl.ds(pl.multiple_of(g * height, height), height)
        for t in range(slots):
            x_ref[dest, t * LANES : (t + 1) * LANES] = got_ref[g * slots + t]
        return carry

    lax.fori_loop(0, groups, place, 0)

    row_block = x_ref.shape[0] // rows
    col_block = x_ref.shape[0] // cols
    upper = lax.broadcasted_iota(jnp.int32, (row_block, LANES), 1) >= half
    for n, dy in enumerate(shifts):
        first = pl.multiple_of(lax.rem(row + dy, rows) * row_block, row_block)
        for t in range(slots):
            lanes = slice(t * LANES, (t + 1) * LANES)
            value = x_ref[pl.ds(first, row_block), lanes]
            turned = pltpu.roll(value.astype(jnp.float32), half, 1)
            l_ref[:row_block, lanes] = value
            l_ref[row_block:, lanes] = jnp.where(upper, -turned, turned).astype(jnp.bfloat16)
        for d in range(cols):
            block = pl.multiple_of(lax.rem(col + d, cols) * col_block, col_block)
            right = x_ref[pl.ds(block, col_block), :]
            value = lax.dot_general(l_ref[...], right, NT, preferred_element_type=jnp.float32) * scale
            for p in range(2):
                outs[n * cols + d][p] = value[p * row_block : (p + 1) * row_block].astype(jnp.bfloat16)


def correlate(at, got, groups, rows, cols, shifts, scale):
    total = groups * got.shape[1]
    depth = rows * cols * LANES
    row_block, col_block = total // rows, total // cols
    piece = jax.ShapeDtypeStruct((2, row_block, col_block), jnp.bfloat16)
    count = len(shifts) * cols
    return pl.pallas_call(
        functools.partial(correlate_kernel, groups, rows, cols, shifts, scale),
        out_shape=[piece] * count,
        in_specs=[SMEM, VMEM],
        out_specs=[VMEM] * count,
        scratch_shapes=[pltpu.VMEM((total, depth), jnp.bfloat16), pltpu.VMEM((2 * row_block, depth), jnp.bfloat16)],
        compiler_params=params(),
        cost_estimate=cost(4 * count * row_block * col_block * depth, 2 * total * depth + 2 * count * piece.size),
        name="correlate",
    )(at, got)


def widen_kernel(count, where_ref, *refs):
    pieces, (o_ref, narrow_ref, wide_ref, in_sems, out_sems) = refs[-count - 5 : -5], refs[-5:]
    reads = [pltpu.make_async_copy(piece, narrow_ref.at[j], in_sems.at[j]) for j, piece in enumerate(pieces)]
    for read in reads:
        read.start()
    writes = []
    for j, read in enumerate(reads):
        read.wait()
        wide_ref[j] = narrow_ref[j].astype(jnp.float32)
        writes.append(pltpu.make_async_copy(wide_ref.at[j], o_ref.at[where_ref[j]], out_sems.at[j]))
        writes[-1].start()
    for write in writes:
        write.wait()


def widen(pieces, where, shape, into=None):
    count, piece = len(pieces), pieces[0]
    before = [] if into is None else [into]
    anywhere = pl.BlockSpec(memory_space=pl.ANY)
    return pl.pallas_call(
        functools.partial(widen_kernel, count),
        in_specs=[SMEM] + [anywhere] * (len(before) + count),
        out_specs=anywhere,
        out_shape=jax.ShapeDtypeStruct(shape, jnp.float32),
        scratch_shapes=[
            pltpu.VMEM((count, *piece.shape), piece.dtype),
            pltpu.VMEM((count, *piece.shape), jnp.float32),
            pltpu.SemaphoreType.DMA((count,)),
            pltpu.SemaphoreType.DMA((count,)),
        ],
        input_output_aliases={1: 0} if before else {},
        compiler_params=params(8),
        cost_estimate=cost(count * piece.size, 6 * count * piece.size),
        name="widen",
    )(where, *before, *pieces)


def per_device(voltages):
    slot_spectra = voltages.shape[1] // FFT_LEN
    rows = lax.axis_size("row")
    cols = lax.axis_size("col")
    slots = rows * cols
    groups = lax.axis_size("chan")
    tail = voltages[:, (slot_spectra - TAPS + 1) * FFT_LEN :]
    earlier = lax.ppermute(tail, ("row", "col"), [(i, i + 1) for i in range(slots - 1)])
    row, col = lax.axis_index("row"), lax.axis_index("col")
    at = jnp.stack([row, col]).astype(jnp.int32)
    scale = 1.0 / (slot_spectra * slots)
    total = groups * voltages.shape[0]
    shape = (slots, 2, total // rows, total // cols)
    message = channelize(voltages, earlier)
    turned = lax.all_to_all(message, ALL, split_axis=0, concat_axis=0, tiled=True)

    def travel(piece, dy, d):
        links = [(r * cols + c, (r + dy) % rows * cols + (c + d) % cols) for r in range(rows) for c in range(cols)]
        return piece if dy == d == 0 else lax.ppermute(piece, ("row", "col"), links)

    arrived = []
    for shifts in ((1,), (3,), (0, 2)):
        sent = correlate(at, turned, groups, rows, cols, shifts, scale)
        turned, sent = lax.optimization_barrier((turned, sent))
        for n, dy in enumerate(shifts):
            for d in range(cols):
                channel = (row + rows - dy) % rows * cols + (col + cols - d) % cols
                arrived.append((travel(sent[n * cols + d], dy, d), channel))
    out = None
    for batch in ((0, 1, 4), (2, 3, 5), (6,), (7,)):
        where = jnp.stack([arrived[b][1] for b in batch]).astype(jnp.int32)
        out = widen([arrived[b][0] for b in batch], where, shape, out)
    return out


def solution(mesh):
    return jax.shard_map(
        per_device,
        mesh=mesh,
        in_specs=(P("chan", ("row", "col")),),
        out_specs=P("chan", None, "row", "col"),
        check_vma=False,
    )
```
